128 devices in a mesh: req: 32 (over z, x, core), mlp: 4 (over y).
Axes of the slice: x: 4, y: 4, z: 4, core: 2. Of those that a mesh axis runs over, the one named last changes fastest.
Arguments:
- residual_in: bfloat16 [32768, 1664], P('req'), may hold values from -6 to 6
- lengths: int32 [4096], P(('req', 'mlp')), may hold values from 0 to 16, as said below
- owners: int32 [4096], P(('req', 'mlp')), may hold values from 0 to 31, as said below
- merge_dest: int32 [32768], P('req'), may hold values from 0 to 255, as said below
- segment_ids: int32 [32768], P('req'), may hold values from 0 to 3, as said below
- norm2_gain: float32 [1664], replicated, may hold values from 0.5 to 1.5
- norm2_bias: float32 [1664], replicated, may hold values from -3 to 3
- up_weight: bfloat16 [4096, 1664], P('mlp'), may hold values from -0.15625 to 0.15625
- up_bias: float32 [4096], P('mlp'), may hold values from -3 to 3
- down_weight: bfloat16 [4096, 1664], P('mlp'), may hold values from -0.09375 to 0.09375
- down_bias: float32 [1664], replicated, may hold values from -3 to 3
- proj_weight: bfloat16 [6656, 1664], P('mlp'), may hold values from -0.078125 to 0.078125
- norm3_gain: float32 [1664], replicated, may hold values from 0.5 to 1.5
- norm3_bias: float32 [1664], replicated, may hold values from -3 to 3
- next_weight: bfloat16 [1664, 3, 1664], P('req'), may hold values from -0.15625 to 0.15625
Outputs:
- merged_out: bfloat16 [16384, 1664], P(('req', 'mlp'))
- next_mixed: bfloat16 [16384, 1664], P(('req', 'mlp'))
The draws below stay inside these ranges and needn't reach their ends.
Inputs may be any that keep to these rules, and one draw needn't show every extreme that they name: The 32 pieces of each block of 256 tokens (one device, req-major order) have lengths that are multiples of 4 and sum to 256; in every block one piece has exactly 16 tokens. The owners of the 32 pieces of one block are a permutation of 0 to 31; for each index of mlp, one piece of 16 tokens of each block of that index goes to one owner shared by all blocks of that index. `merge_dest`: within each device block a permutation of 0 to 255 that maps the tokens of each piece onto that piece's own positions. `segment_ids`: the four tokens of a block whose merge_dest values have the same quotient by 4 carry one segment id.
All inputs are finite; a program needn't handle non-finite values.
Results may differ from the reference program's by a relative error of at most 0.023.
Values may be sent and summed in bfloat16 or wider, within the bound.
No kernel may reach another device: no remote copies, remote signals or barrier semaphores. Data moves between devices by JAX's collectives and lax.ppermute only.
A program may use at most 128 MiB of HBM per device.

```python
import math
import jax
import jax.numpy as jnp
from jax import lax

D = 1664
HEADS = 16
HEAD_DIM = 104
FF = 4096
TOK_DEV = 256
SEGS = 4
SLOTS = 4
TOKENS = 32768
N_REQ = 32
N_MLP = 4
DEVICES = 128


def shuffle_rows(key_base, count, length):

    def one_row(row_key):
        return jax.random.permutation(row_key, length)
    return jax.vmap(one_row)(jax.random.split(key_base, count))


def request_layout(key):
    base_key = jax.random.fold_in(key, 4321)
    key_fill, key_order, key_merge, key_owner, key_mark, key_full = jax.random.split(base_key, 6)
    unit_count = TOK_DEV // 4
    slot_count = TOK_DEV // (2 * N_REQ)
    cell_count = (N_REQ - 1) * slot_count
    taken = unit_count - slot_count
    cell_ranks = shuffle_rows(key_fill, DEVICES, cell_count)
    chosen = (cell_ranks < taken).astype(jnp.int32).reshape(DEVICES, N_REQ - 1, slot_count)
    bins = jnp.concatenate([jnp.full((DEVICES, 1), slot_count, jnp.int32), jnp.sum(chosen, axis=2).astype(jnp.int32)], axis=1)
    piece_order = shuffle_rows(key_order, DEVICES, N_REQ).astype(jnp.int32)
    units = jnp.take_along_axis(bins, piece_order, axis=1)
    lengths = 4 * units
    piece_ids = jnp.arange(N_REQ, dtype=jnp.int32)
    full_index = jnp.sum(piece_ids[None, :] * (piece_order == 0).astype(jnp.int32), axis=1)
    starts = jnp.cumsum(lengths, axis=1) - lengths
    positions = jnp.arange(TOK_DEV, dtype=jnp.int32)
    piece_of = jnp.sum((positions[None, :, None] >= starts[:, None, :]).astype(jnp.int32), axis=2) - 1
    shuffle = shuffle_rows(key_merge, DEVICES, TOK_DEV).astype(jnp.int32)
    token_order = jnp.argsort(piece_of * TOK_DEV + shuffle, axis=1)
    merge_places = jnp.argsort(token_order, axis=1).astype(jnp.int32)
    row_marks = jax.random.randint(key_mark, (DEVICES, unit_count), 0, SEGS).astype(jnp.int32)
    token_marks = jnp.take_along_axis(row_marks, merge_places // 4, axis=1)
    permuted = shuffle_rows(key_owner, DEVICES, N_REQ).astype(jnp.int32)
    lane_owner = jax.random.randint(key_full, (N_MLP,), 0, N_REQ).astype(jnp.int32)
    device_lane = jnp.arange(DEVICES, dtype=jnp.int32) % N_MLP
    wanted = jnp.take(lane_owner, device_lane)
    wanted_at = jnp.sum(piece_ids[None, :] * (permuted == wanted[:, None]).astype(jnp.int32), axis=1)
    value_at_full = jnp.sum(permuted * (piece_ids[None, :] == full_index[:, None]).astype(jnp.int32), axis=1)
    owner_rows = jnp.where(piece_ids[None, :] == full_index[:, None], wanted[:, None], jnp.where(piece_ids[None, :] == wanted_at[:, None], value_at_full[:, None], permuted))
    return (lengths.astype(jnp.int32), owner_rows.astype(jnp.int32), merge_places, token_marks.astype(jnp.int32))


def draw_lengths(key, part):
    return request_layout(key)[0].reshape(DEVICES * N_REQ)


def draw_owners(key, part):
    return request_layout(key)[1].reshape(DEVICES * N_REQ)


def draw_merge_dest(key, part):
    return request_layout(key)[2].reshape(DEVICES * TOK_DEV)


def draw_segment_ids(key, part):
    return request_layout(key)[3].reshape(DEVICES * TOK_DEV)


def block_scale(stream_key, extent, cuts, least, high):
    def one(position, blocks):
        draws = jax.random.uniform(jax.random.fold_in(jax.random.fold_in(stream_key, 6), position), (blocks,), jnp.float32, least / len(cuts), high / len(cuts))
        return jnp.repeat(jnp.exp(draws), extent[position] // blocks).reshape((-1,) + (1,) * (len(extent) - position - 1))

    loudness = one(*cuts[0])
    for cut in cuts[1:]:
        loudness = loudness * one(*cut)
    return loudness


def gaussian(own_key, shape, deviation, reach, cuts=(), kind=jnp.bfloat16):
    drawn = deviation * jax.random.normal(own_key, shape, jnp.float32)
    if cuts:
        drawn = drawn * block_scale(own_key, shape, cuts, -0.22, 0.18)
    return jnp.clip(drawn, -reach, reach).astype(kind)


def setup_inputs(seed: int = 0) -> dict:
    key_of = jax.random.split(jax.random.key(seed), 16)
    residual_in = gaussian(key_of[0], (TOKENS, D), 1.0, 6.0, ((0, 32),))
    lengths = draw_lengths(jax.random.fold_in(key_of[15], 71), 0)
    owners = draw_owners(jax.random.fold_in(key_of[15], 71), 0)
    merge_dest = draw_merge_dest(jax.random.fold_in(key_of[15], 71), 0)
    segment_ids = draw_segment_ids(jax.random.fold_in(key_of[15], 71), 0)
    norm2_gain = jnp.clip(1.0 + 0.1 * jax.random.normal(key_of[5], (D,), jnp.float32), 0.5, 1.5)
    norm2_bias = gaussian(key_of[6], (D,), 0.5, 3.0, (), jnp.float32)
    up_weight = gaussian(key_of[7], (FF, D), D ** -0.5, 0.15625, ((0, 4),))
    up_bias = gaussian(key_of[8], (FF,), 0.5, 3.0, ((0, 4),), jnp.float32)
    down_weight = gaussian(key_of[9], (FF, D), FF ** -0.5, 0.09375, ((0, 4),))
    down_bias = gaussian(key_of[10], (D,), 0.5, 3.0, (), jnp.float32)
    proj_weight = gaussian(key_of[11], (4 * D, D), (4 * D) ** -0.5, 0.078125, ((0, 4),))
    norm3_gain = jnp.clip(1.0 + 0.1 * jax.random.normal(key_of[12], (D,), jnp.float32), 0.5, 1.5)
    norm3_bias = gaussian(key_of[13], (D,), 0.5, 3.0, (), jnp.float32)
    next_weight = gaussian(key_of[14], (D, 3, D), D ** -0.5, 0.15625, ((0, 32),))
    return {"residual_in": residual_in, "lengths": lengths, "owners": owners, "merge_dest": merge_dest, "segment_ids": segment_ids, "norm2_gain": norm2_gain, "norm2_bias": norm2_bias, "up_weight": up_weight, "up_bias": up_bias, "down_weight": down_weight, "down_bias": down_bias, "proj_weight": proj_weight, "norm3_gain": norm3_gain, "norm3_bias": norm3_bias, "next_weight": next_weight}


EPSILON = 1e-06

def layer_norm(rows, gain, bias):
    values = rows.astype(jnp.float32)
    mean_value = lax.optimization_barrier(jnp.mean(values, axis=-1, keepdims=True))
    centred = values - mean_value
    spread = lax.optimization_barrier(jnp.mean(centred * centred, axis=-1, keepdims=True))
    return centred * lax.rsqrt(spread + EPSILON) * gain + bias

def block_attention(pair):
    heads_block, tag_block = pair
    queries = heads_block[:, 0].astype(jnp.float32)
    key_rows = heads_block[:, 1].astype(jnp.float32)
    value_rows = heads_block[:, 2].astype(jnp.float32)
    score_scale = 1.0 / math.sqrt(heads_block.shape[-1])
    scores = jnp.einsum('qhe,khe->hqk', queries, key_rows) * score_scale
    slot_total = heads_block.shape[0]
    itself = lax.broadcasted_iota(jnp.int32, (slot_total, slot_total), 0) == lax.broadcasted_iota(jnp.int32, (slot_total, slot_total), 1)
    live_slots = tag_block >= 0
    same_request = tag_block[:, None] == tag_block[None, :]
    allowed = same_request & live_slots[None, :] | itself
    weights = jnp.where(allowed[None], jnp.exp(scores), 0.0)
    probs = (weights / lax.optimization_barrier(jnp.sum(weights, axis=-1, keepdims=True))).astype(jnp.bfloat16)
    mixed_out = jnp.einsum('hqk,khe->qhe', probs.astype(jnp.float32), value_rows)
    mixed_out = jnp.where(live_slots[:, None, None], mixed_out, 0.0)
    return mixed_out.astype(jnp.bfloat16)

def reference(residual_in, lengths, owners, merge_dest, segment_ids, norm2_gain, norm2_bias, up_weight, up_bias, down_weight, down_bias, proj_weight, norm3_gain, norm3_bias, next_weight):
    group_rows = TOK_DEV * N_MLP

    def feed_group(rows):
        normed = layer_norm(rows, norm2_gain, norm2_bias).astype(jnp.bfloat16)
        upward = lax.dot_general(normed, up_weight, (((1,), (1,)), ((), ())), preferred_element_type=jnp.float32)
        hidden = jax.nn.gelu(upward + up_bias, approximate=False).astype(jnp.bfloat16)
        feed_out = jnp.dot(hidden, down_weight, preferred_element_type=jnp.float32)
        return (rows.astype(jnp.float32) + feed_out + down_bias).astype(jnp.bfloat16)
    layer_out = lax.map(feed_group, residual_in.reshape(N_REQ, group_rows, D))
    blocks = layer_out.reshape(DEVICES, TOK_DEV, D)
    places = merge_dest.reshape(DEVICES, TOK_DEV)
    marks = segment_ids.reshape(DEVICES, TOK_DEV)

    def merge_block(triple):
        rows, dest_block, mark_block = triple
        source = jnp.zeros((TOK_DEV,), jnp.int32).at[dest_block].set(jnp.arange(TOK_DEV, dtype=jnp.int32))
        merged_rows = jnp.take(rows, source, axis=0).reshape(TOK_DEV // 4, 4 * D)
        row_segment = jnp.take(mark_block, source.reshape(TOK_DEV // 4, 4)[:, 0], axis=0)
        return (merged_rows, row_segment)
    merged, row_segment = lax.map(merge_block, (blocks, places, marks))
    merged = merged.reshape(DEVICES * (TOK_DEV // 4), 4 * D)
    projected = jnp.dot(merged, proj_weight, preferred_element_type=jnp.float32).astype(jnp.bfloat16)
    per_device = TOK_DEV // 4
    counts = (lengths // 4).reshape(DEVICES, N_REQ)
    starts = jnp.cumsum(counts, axis=1) - counts
    index = jnp.arange(per_device, dtype=jnp.int32)
    inside = ((index[None, :, None] >= starts[:, None, :]) & (index[None, :, None] < (starts + counts)[:, None, :])).astype(jnp.int32)
    piece_owner = owners.reshape(DEVICES, N_REQ)
    owner_of = lax.optimization_barrier(jnp.sum(inside * piece_owner[:, None, :], axis=2))
    rank = index[None, :] - lax.optimization_barrier(jnp.sum(inside * starts[:, None, :], axis=2))
    device = jnp.arange(DEVICES, dtype=jnp.int32)
    sender = device // N_MLP
    lane_of = device % N_MLP
    recv_rows = N_REQ * SLOTS
    target = (owner_of * N_MLP + lane_of[:, None]) * recv_rows + sender[:, None] * SLOTS + rank
    merged_out = jnp.zeros((DEVICES * recv_rows, D), jnp.bfloat16).at[target.reshape(-1)].set(projected)
    slot_segment = jnp.full((DEVICES * recv_rows,), -1, jnp.int32).at[target.reshape(-1)].set(row_segment.reshape(-1))
    normed3 = layer_norm(merged_out, norm3_gain, norm3_bias).astype(jnp.bfloat16)
    heads_in = jnp.dot(normed3, next_weight.reshape(D, 3 * D), preferred_element_type=jnp.float32).astype(jnp.bfloat16)
    heads_in = heads_in.reshape(DEVICES, recv_rows, 3, HEADS, HEAD_DIM)
    next_mixed = lax.map(block_attention, (heads_in, slot_segment.reshape(DEVICES, recv_rows)))
    return (merged_out, next_mixed.reshape(DEVICES * recv_rows, D))
```

```python
import math

import jax
import jax.numpy as jnp
from jax import lax
from jax.experimental import pallas as pl
from jax.experimental.pallas import tpu as pltpu
from jax.sharding import PartitionSpec as P

HEAD_DIM = 104
EPSILON = 1e-06
MIB = 1 << 20


def normalise(values, gain, bias):
    mean_value = jnp.mean(values, axis=-1, keepdims=True)
    centred = values - mean_value
    spread = jnp.mean(centred * centred, axis=-1, keepdims=True)
    return centred * lax.rsqrt(spread + EPSILON) * gain + bias


def relative_offset(step):
    return jnp.where(step == 0, 2, jnp.where(step == 1, 1, jnp.where(step == 2, 3, 0)))


def arrange_kernel(lane_ref, rows_ref, dest_ref, gain_ref, bias_ref, normed_ref, own_ref):
    lane = lane_ref[0]
    rows = rows_ref[...]
    count = rows.shape[0]
    part = count // 4
    normed = normalise(rows.astype(jnp.float32), gain_ref[...], bias_ref[...]).astype(jnp.bfloat16)
    index = lax.broadcasted_iota(jnp.int32, (count, count), 0)
    step = index // part
    wanted = 4 * (index - step * part) + ((lane + relative_offset(step)) & 3)
    hits = jnp.where(dest_ref[0] == wanted, 1.0, 0.0).astype(jnp.bfloat16)
    moved = jnp.dot(hits, normed, preferred_element_type=jnp.float32).astype(jnp.bfloat16)
    normed_ref[...] = moved.reshape(normed_ref.shape)
    own = jnp.dot(hits[3 * part :], rows, preferred_element_type=jnp.float32).astype(jnp.bfloat16)
    own_ref[...] = own.reshape(own_ref.shape)


def arrange(lane, residual_in, merge_dest, gain, bias):
    group_rows, width = residual_in.shape
    block = group_rows // 4
    part = block // 4
    return pl.pallas_call(
        arrange_kernel,
        grid_spec=pltpu.PrefetchScalarGridSpec(
            num_scalar_prefetch=1,
            grid=(4,),
            in_specs=[
                pl.BlockSpec((block, width), lambda b, s: (b, 0)),
                pl.BlockSpec((1, 1, block), lambda b, s: (b, 0, 0)),
                pl.BlockSpec((1, width), lambda b, s: (0, 0)),
                pl.BlockSpec((1, width), lambda b, s: (0, 0)),
            ],
            out_specs=[
                pl.BlockSpec((4, 1, part, width), lambda b, s: (0, b, 0, 0)),
                pl.BlockSpec((1, part, width), lambda b, s: (b, 0, 0)),
            ],
        ),
        out_shape=[
            jax.ShapeDtypeStruct((4, 4, part, width), jnp.bfloat16),
            jax.ShapeDtypeStruct((4, part, width), jnp.bfloat16),
        ],
        compiler_params=pltpu.CompilerParams(vmem_limit_bytes=24 * MIB),
        name="arrange",
    )(lane, residual_in, merge_dest.reshape(4, 1, block), gain, bias)


def gelu(value):
    return 0.5 * value * (1.0 + lax.erf(value * (1.0 / math.sqrt(2.0))))


def feed_step(rows_ref, up_ref, up_bias_ref, down_ref, total_ref):
    upward = lax.dot_general(
        rows_ref[...], up_ref[...], (((1,), (1,)), ((), ())), preferred_element_type=jnp.float32
    )
    hidden = gelu(upward + up_bias_ref[...]).astype(jnp.bfloat16)
    part = jnp.dot(hidden, down_ref[...], preferred_element_type=jnp.float32)

    @pl.when(pl.program_id(0) == 0)
    def _():
        total_ref[...] = part

    @pl.when(pl.program_id(0) > 0)
    def _():
        total_ref[...] += part


def feed_kernel(rows_ref, up_ref, up_bias_ref, down_ref, first_ref, second_ref, total_ref):
    feed_step(rows_ref, up_ref, up_bias_ref, down_ref, total_ref)

    @pl.when(pl.program_id(0) == pl.num_programs(0) - 1)
    def _():
        half = first_ref.shape[0]
        first_ref[...] = total_ref[:half].astype(jnp.bfloat16)
        second_ref[...] = total_ref[half:].astype(jnp.bfloat16)


def feed_own_kernel(
    rows_ref, up_ref, up_bias_ref, down_ref, residual_ref, down_bias_ref, out_ref, total_ref
):
    feed_step(rows_ref, up_ref, up_bias_ref, down_ref, total_ref)

    @pl.when(pl.program_id(0) == pl.num_programs(0) - 1)
    def _():
        out_ref[...] = total_ref[...] + (
            residual_ref[...].astype(jnp.float32) + down_bias_ref[...]
        )


def feed(rows, step, up_weight, up_bias, down_weight, extra=None):
    _, count, width = rows.shape
    hidden_units = up_weight.shape[0]
    tile = 256
    in_specs = [
        pl.BlockSpec((None, count, width), lambda j: (step, 0, 0)),
        pl.BlockSpec((tile, width), lambda j: (j, 0)),
        pl.BlockSpec((1, tile), lambda j: (0, j)),
        pl.BlockSpec((tile, width), lambda j: (j, 0)),
    ]
    args = [rows, up_weight, up_bias, down_weight]
    if extra is None:
        half = count // 2
        out_specs = [pl.BlockSpec((half, width), lambda j: (0, 0))] * 2
        out_shape = [jax.ShapeDtypeStruct((half, width), jnp.bfloat16)] * 2
        kernel = feed_kernel
    else:
        in_specs += [
            pl.BlockSpec((count, width), lambda j: (0, 0)),
            pl.BlockSpec((1, width), lambda j: (0, 0)),
        ]
        args += list(extra)
        out_specs = pl.BlockSpec((count, width), lambda j: (0, 0))
        out_shape = jax.ShapeDtypeStruct((count, width), jnp.float32)
        kernel = feed_own_kernel
    return pl.pallas_call(
        kernel,
        grid=(hidden_units // tile,),
        in_specs=in_specs,
        out_specs=out_specs,
        out_shape=out_shape,
        scratch_shapes=[pltpu.VMEM((count, width), jnp.float32)],
        compiler_params=pltpu.CompilerParams(vmem_limit_bytes=24 * MIB),
        cost_estimate=pl.CostEstimate(
            flops=4 * count * width * hidden_units,
            bytes_accessed=4 * hidden_units * width + 8 * count * width,
            transcendentals=count * hidden_units,
        ),
        name="feed",
    )(*args)


def project_kernel(
    lane_ref, base_ref, a1_ref, a2_ref, b1_ref, b2_ref, weight_ref, o0, o1, o2, own, total_ref
):
    half = a1_ref.shape[0]
    part = half // 2
    top = base_ref[:half] + a1_ref[...].astype(jnp.float32) + a2_ref[...].astype(jnp.float32)
    low = base_ref[half:] + b1_ref[...].astype(jnp.float32) + b2_ref[...].astype(jnp.float32)
    rows = jnp.concatenate([top, low], axis=0).astype(jnp.bfloat16)
    total_ref[...] = jnp.dot(rows, weight_ref[...], preferred_element_type=jnp.float32)
    lane = lane_ref[0]
    for offset, ref in ((2, o0), (1, o1), (3, o2), (0, own)):
        start = pl.multiple_of(((lane + offset) & 3) * part, part)
        ref[...] = total_ref[pl.ds(start, part)].astype(ref.dtype)


def project(lane, base, a1, a2, b1, b2, weight):
    count, width = base.shape
    part = count // 4
    vmem = pl.BlockSpec(memory_space=pltpu.VMEM)
    return pl.pallas_call(
        project_kernel,
        in_specs=[pl.BlockSpec(memory_space=pltpu.SMEM)] + [vmem] * 6,
        out_specs=[vmem] * 4,
        out_shape=[jax.ShapeDtypeStruct((part, width), jnp.bfloat16)] * 3
        + [jax.ShapeDtypeStruct((part, width), jnp.float32)],
        scratch_shapes=[pltpu.VMEM((count, width), jnp.float32)],
        compiler_params=pltpu.CompilerParams(vmem_limit_bytes=24 * MIB),
        cost_estimate=pl.CostEstimate(
            flops=2 * count * width * width,
            bytes_accessed=2 * width * width + 12 * count * width,
            transcendentals=0,
        ),
        name="project",
    )(lane, base, a1, a2, b1, b2, weight)


def turn(column):
    count = column.shape[0]
    same = lax.broadcasted_iota(jnp.int32, (count, count), 0) == lax.broadcasted_iota(
        jnp.int32, (count, count), 1
    )
    return jnp.sum(jnp.where(same, column, 0), axis=0, keepdims=True)


def route_kernel(
    lane_ref, own_ref, r0, r1, r2, counts_ref, owners_ref, dest_ref, seg_ref, out_ref
):
    lane = lane_ref[0]
    rows, width = own_ref.shape
    pieces = counts_ref.shape[1]
    slots = 2 * rows // pieces
    projected = (
        own_ref[...]
        + r0[...].astype(jnp.float32)
        + r1[...].astype(jnp.float32)
        + r2[...].astype(jnp.float32)
    ).astype(jnp.bfloat16)
    counts = counts_ref[...] // 4
    earlier = lax.broadcasted_iota(jnp.int32, (pieces, pieces), 1) < lax.broadcasted_iota(
        jnp.int32, (pieces, pieces), 0
    )
    starts = jnp.sum(jnp.where(earlier, counts, 0), axis=1, keepdims=True)
    upto = earlier | (
        lax.broadcasted_iota(jnp.int32, (pieces, pieces), 1)
        == lax.broadcasted_iota(jnp.int32, (pieces, pieces), 0)
    )
    ends = jnp.sum(jnp.where(upto, counts, 0), axis=1, keepdims=True)
    index = lax.broadcasted_iota(jnp.int32, (pieces, rows), 1)
    inside = (index >= starts) & (index < ends)
    owner_col = jnp.sum(
        jnp.where(
            lax.broadcasted_iota(jnp.int32, (pieces, pieces), 0)
            == lax.broadcasted_iota(jnp.int32, (pieces, pieces), 1),
            owners_ref[...],
            0,
        ),
        axis=1,
        keepdims=True,
    )
    target = jnp.sum(jnp.where(inside, owner_col * slots - starts, 0), axis=0, keepdims=True)
    target = target + lax.broadcasted_iota(jnp.int32, (1, rows), 1)
    out_rows = pieces * slots
    hits = lax.broadcasted_iota(jnp.int32, (out_rows, rows), 0) == target
    moved = jnp.dot(
        jnp.where(hits, 1.0, 0.0).astype(jnp.bfloat16),
        projected,
        preferred_element_type=jnp.float32,
    ).astype(jnp.bfloat16)
    dest = dest_ref[lane]
    seg = seg_ref[lane]
    tokens = dest.shape[1]
    first = dest == 4 * lax.broadcasted_iota(jnp.int32, (rows, tokens), 0)
    marks = turn(jnp.sum(jnp.where(first, seg, 0), axis=1, keepdims=True)) + 1
    tags = jnp.sum(jnp.where(hits, marks, 0), axis=1, keepdims=True)
    out_ref[:, :width] = moved
    out_ref[:, width:] = jnp.broadcast_to(
        tags.astype(jnp.float32), (out_rows, out_ref.shape[1] - width)
    ).astype(jnp.bfloat16)


def route(lane, own, others, lengths, owners, merge_dest, segment_ids):
    rows, width = own.shape
    pieces = lengths.shape[0]
    block = merge_dest.shape[0] // 4
    vmem = pl.BlockSpec(memory_space=pltpu.VMEM)
    return pl.pallas_call(
        route_kernel,
        in_specs=[pl.BlockSpec(memory_space=pltpu.SMEM)] + [vmem] * 8,
        out_specs=vmem,
        out_shape=jax.ShapeDtypeStruct((2 * rows, width + 128), jnp.bfloat16),
        compiler_params=pltpu.CompilerParams(vmem_limit_bytes=24 * MIB),
        name="route",
    )(
        lane,
        own,
        *others,
        lengths.reshape(1, pieces),
        owners.reshape(1, pieces),
        merge_dest.reshape(4, 1, block),
        segment_ids.reshape(4, 1, block),
    )


def attend_kernel(got_ref, gain_ref, bias_ref, weight_ref, merged_ref, mixed_ref, heads_ref):
    count, width = merged_ref.shape
    rows = got_ref[:, :width]
    merged_ref[...] = rows
    tags = got_ref[:, width:].astype(jnp.float32)
    tag_col = tags[:, :1]
    itself = lax.broadcasted_iota(jnp.int32, (count, count), 0) == lax.broadcasted_iota(
        jnp.int32, (count, count), 1
    )
    tag_row = jnp.sum(jnp.where(itself, tag_col, 0.0), axis=0, keepdims=True)
    allowed = ((tag_col == tag_row) & (tag_row > 0.5)) | itself
    live = tag_col > 0.5
    normed = normalise(rows.astype(jnp.float32), gain_ref[...], bias_ref[...]).astype(jnp.bfloat16)
    heads_ref[...] = jnp.dot(normed, weight_ref[...], preferred_element_type=jnp.float32).astype(
        jnp.bfloat16
    )
    scale = 1.0 / math.sqrt(HEAD_DIM)
    for head in range(width // HEAD_DIM):
        at = head * HEAD_DIM
        query = heads_ref[:, at : at + HEAD_DIM]
        keys = heads_ref[:, width + at : width + at + HEAD_DIM]
        value = heads_ref[:, 2 * width + at : 2 * width + at + HEAD_DIM]
        scores = (
            lax.dot_general(
                query, keys, (((1,), (1,)), ((), ())), preferred_element_type=jnp.float32
            )
            * scale
        )
        weights = jnp.where(allowed, jnp.exp(scores), 0.0)
        probs = (weights / jnp.sum(weights, axis=-1, keepdims=True)).astype(jnp.bfloat16)
        mixed = jnp.dot(probs, value, preferred_element_type=jnp.float32)
        mixed_ref[:, at : at + HEAD_DIM] = jnp.where(live, mixed, 0.0).astype(jnp.bfloat16)


def attend(got, gain, bias, weight):
    count = got.shape[0]
    width, columns = weight.shape
    vmem = pl.BlockSpec(memory_space=pltpu.VMEM)
    return pl.pallas_call(
        attend_kernel,
        in_specs=[vmem] * 4,
        out_specs=[vmem] * 2,
        out_shape=[jax.ShapeDtypeStruct((count, width), jnp.bfloat16)] * 2,
        scratch_shapes=[pltpu.VMEM((count, columns), jnp.bfloat16)],
        compiler_params=pltpu.CompilerParams(vmem_limit_bytes=32 * MIB),
        cost_estimate=pl.CostEstimate(
            flops=2 * count * width * columns,
            bytes_accessed=2 * width * columns,
            transcendentals=count * count * 16,
        ),
        name="attend",
    )(got, gain, bias, weight)


def body(
    residual_in,
    lengths,
    owners,
    merge_dest,
    segment_ids,
    norm2_gain,
    norm2_bias,
    up_weight,
    up_bias,
    down_weight,
    down_bias,
    proj_weight,
    norm3_gain,
    norm3_bias,
    next_weight,
):
    width = residual_in.shape[1]
    lanes = lax.axis_size("mlp")
    lane = lax.axis_index("mlp").astype(jnp.int32).reshape(1)
    onward = [(i, (i + 1) % lanes) for i in range(lanes)]
    back = [(i, (i - 1) % lanes) for i in range(lanes)]
    across = [(i, (i + 2) % lanes) for i in range(lanes)]

    def row(vector):
        return vector.reshape(1, -1)

    depth = next_weight.shape[0]
    padded = -(-depth // 8) * 8
    shard = jnp.pad(next_weight.reshape(depth, -1), ((0, padded - depth), (0, 0)))
    gathered = lax.all_gather(shard, "req", axis=0, tiled=True)
    full = gathered.reshape(-1, padded, 3 * width)[:, :depth].reshape(width, 3 * width)

    normed, own_rows = arrange(lane, residual_in, merge_dest, row(norm2_gain), row(norm2_bias))
    count = residual_in.shape[0] // lanes
    normed = normed.reshape(4, count, width)
    bias_up = row(up_bias)
    far_a, far_b = feed(normed, 0, up_weight, bias_up, down_weight)
    far_a = lax.ppermute(far_a, "mlp", onward)
    far_b = lax.ppermute(far_b, "mlp", back)
    next_a, next_b = feed(normed, 1, up_weight, bias_up, down_weight)
    b1 = lax.ppermute(next_b, "mlp", onward)
    prev_a, prev_b = feed(normed, 2, up_weight, bias_up, down_weight)
    a2 = lax.ppermute(prev_a, "mlp", back)

    def join(first, second):
        return (first.astype(jnp.float32) + second.astype(jnp.float32)).astype(jnp.bfloat16)

    a1 = lax.ppermute(join(far_a, next_a), "mlp", onward)
    b2 = lax.ppermute(join(far_b, prev_b), "mlp", back)
    base = feed(
        normed,
        3,
        up_weight,
        bias_up,
        down_weight,
        (own_rows.reshape(count, width), row(down_bias)),
    )
    p0, p1, p2, own = project(lane, base, a1, a2, b1, b2, proj_weight)
    others = (
        lax.ppermute(p0, "mlp", across),
        lax.ppermute(p1, "mlp", onward),
        lax.ppermute(p2, "mlp", back),
    )
    outgoing = route(lane, own, others, lengths, owners, merge_dest, segment_ids)
    got = lax.all_to_all(outgoing, "req", split_axis=0, concat_axis=0, tiled=True)
    return tuple(attend(got, row(norm3_gain), row(norm3_bias), full))


def solution(mesh):
    return jax.shard_map(
        body,
        mesh=mesh,
        in_specs=(
            P("req", None),
            P(("req", "mlp")),
            P(("req", "mlp")),
            P("req"),
            P("req"),
            P(),
            P(),
            P("mlp", None),
            P("mlp"),
            P("mlp", None),
            P(),
            P("mlp", None),
            P(),
            P(),
            P("req", None, None),
        ),
        out_specs=(P(("req", "mlp"), None), P(("req", "mlp"), None)),
        check_vma=False,
    )
```

```python
import math

import jax
import jax.numpy as jnp
from jax import lax
from jax.experimental import pallas as pl
from jax.experimental.pallas import tpu as pltpu
from jax.sharding import PartitionSpec as P

HEAD_DIM = 104
EPSILON = 1e-06
MIB = 1 << 20


def normalise(values, gain, bias):
    mean_value = jnp.mean(values, axis=-1, keepdims=True)
    centred = values - mean_value
    spread = jnp.mean(centred * centred, axis=-1, keepdims=True)
    return centred * lax.rsqrt(spread + EPSILON) * gain + bias


def relative_offset(step):
    return jnp.where(step == 0, 2, jnp.where(step == 1, 1, jnp.where(step == 2, 3, 0)))


def gelu(value):
    return 0.5 * value * (1.0 + lax.erf(value * (1.0 / math.sqrt(2.0))))


def feed_tiles(rows, up_ref, up_bias_ref, down_ref, wait=None, tile=256):
    total = None
    for at in range(0, up_ref.shape[0], tile):
        if wait is not None:
            wait(at // tile)
        upward = lax.dot_general(
            rows,
            up_ref[at : at + tile],
            (((1,), (1,)), ((), ())),
            preferred_element_type=jnp.float32,
        )
        hidden = gelu(upward + up_bias_ref[:, at : at + tile]).astype(jnp.bfloat16)
        part = jnp.dot(hidden, down_ref[at : at + tile], preferred_element_type=jnp.float32)
        total = part if total is None else total + part
    return total


def first_kernel(
    lane_ref,
    rows_hbm,
    dest_ref,
    gain_ref,
    bias_ref,
    up_hbm,
    up_bias_ref,
    down_hbm,
    first_ref,
    second_ref,
    normed_ref,
    own_ref,
    rows_ref,
    up_ref,
    down_ref,
    far_ref,
    row_sems,
    up_sems,
    down_sems,
):
    lane = lane_ref[0]
    count = rows_hbm.shape[0] // 4
    part = count // 4
    tile = up_hbm.shape[0] // 4

    def copies(source, target, sems, size):
        return [
            pltpu.make_async_copy(
                source.at[pl.ds(i * size, size)], target.at[pl.ds(i * size, size)], sems.at[i]
            )
            for i in range(4)
        ]

    row_copies = copies(rows_hbm, rows_ref, row_sems, count)
    up_copies = copies(up_hbm, up_ref, up_sems, tile)
    down_copies = copies(down_hbm, down_ref, down_sems, tile)
    for copy in row_copies:
        copy.start()
    for i in range(4):
        up_copies[i].start()
        down_copies[i].start()
    index = lax.broadcasted_iota(jnp.int32, (count, count), 0)
    step = index // part
    wanted = 4 * (index - step * part) + ((lane + relative_offset(step)) & 3)
    for b in range(4):
        row_copies[b].wait()
        rows = rows_ref[b * count : (b + 1) * count]
        normed = normalise(rows.astype(jnp.float32), gain_ref[...], bias_ref[...])
        hits = jnp.where(dest_ref[b] == wanted, 1.0, 0.0).astype(jnp.bfloat16)
        moved = jnp.dot(
            hits, normed.astype(jnp.bfloat16), preferred_element_type=jnp.float32
        ).astype(jnp.bfloat16)
        far_ref[b * part : (b + 1) * part] = moved[:part]
        for k in range(3):
            normed_ref[k, b * part : (b + 1) * part] = moved[(k + 1) * part : (k + 2) * part]
        own_ref[b * part : (b + 1) * part] = jnp.dot(
            hits[3 * part :], rows, preferred_element_type=jnp.float32
        ).astype(jnp.bfloat16)

    def wait(i):
        up_copies[i].wait()
        down_copies[i].wait()

    total = feed_tiles(far_ref[...], up_ref, up_bias_ref, down_ref, wait, tile)
    half = count // 2
    first_ref[...] = total[:half].astype(jnp.bfloat16)
    second_ref[...] = total[half:].astype(jnp.bfloat16)


VMEM = pl.BlockSpec(memory_space=pltpu.VMEM)
SMEM = pl.BlockSpec(memory_space=pltpu.SMEM)
HBM = pl.BlockSpec(memory_space=pltpu.HBM)


def first(lane, residual_in, merge_dest, gain, bias, up_weight, up_bias, down_weight):
    group_rows, width = residual_in.shape
    count = group_rows // 4
    half = count // 2
    bf16 = jnp.bfloat16
    return pl.pallas_call(
        first_kernel,
        in_specs=[SMEM, HBM, VMEM, VMEM, VMEM, HBM, VMEM, HBM],
        out_specs=[VMEM] * 4,
        out_shape=[
            jax.ShapeDtypeStruct((half, width), bf16),
            jax.ShapeDtypeStruct((half, width), bf16),
            jax.ShapeDtypeStruct((3, count, width), bf16),
            jax.ShapeDtypeStruct((count, width), bf16),
        ],
        scratch_shapes=[
            pltpu.VMEM(residual_in.shape, bf16),
            pltpu.VMEM(up_weight.shape, bf16),
            pltpu.VMEM(down_weight.shape, bf16),
            pltpu.VMEM((count, width), bf16),
            pltpu.SemaphoreType.DMA((4,)),
            pltpu.SemaphoreType.DMA((4,)),
            pltpu.SemaphoreType.DMA((4,)),
        ],
        compiler_params=pltpu.CompilerParams(vmem_limit_bytes=32 * MIB),
        cost_estimate=FEED_COST,
        name="first",
    )(lane, residual_in, merge_dest.reshape(4, 1, count), gain, bias, up_weight, up_bias, down_weight)


def feed_kernel(rows_ref, up_ref, up_bias_ref, down_ref, first_ref, second_ref):
    total = feed_tiles(rows_ref[...], up_ref, up_bias_ref, down_ref)
    half = first_ref.shape[0]
    first_ref[...] = total[:half].astype(jnp.bfloat16)
    second_ref[...] = total[half:].astype(jnp.bfloat16)


def feed_own_kernel(
    rows_ref, up_ref, up_bias_ref, down_ref, residual_ref, down_bias_ref, out_ref
):
    total = feed_tiles(rows_ref[...], up_ref, up_bias_ref, down_ref)
    out_ref[...] = total + (residual_ref[...].astype(jnp.float32) + down_bias_ref[...])


FEED_COST = pl.CostEstimate(flops=7 << 28, bytes_accessed=1 << 22, transcendentals=0)


def feed(rows, step, up_weight, up_bias, down_weight, extra=None):
    _, count, width = rows.shape
    args = [rows, up_weight, up_bias, down_weight]
    if extra is None:
        half = count // 2
        out_shape = [jax.ShapeDtypeStruct((half, width), jnp.bfloat16)] * 2
        kernel = feed_kernel
    else:
        args += list(extra)
        out_shape = jax.ShapeDtypeStruct((count, width), jnp.float32)
        kernel = feed_own_kernel

    def wrapped(rows_ref, *refs):
        kernel(rows_ref.at[step], *refs)

    return pl.pallas_call(
        wrapped,
        in_specs=[VMEM] * len(args),
        out_specs=[VMEM] * 2 if extra is None else VMEM,
        out_shape=out_shape,
        compiler_params=pltpu.CompilerParams(vmem_limit_bytes=16 * MIB),
        cost_estimate=FEED_COST,
        name="feed",
    )(*args)


def project_kernel(
    lane_ref, base_ref, a1_ref, a2_ref, b1_ref, b2_ref, weight_ref, o0, o1, o2, own, total_ref
):
    half = a1_ref.shape[0]
    part = half // 2
    top = base_ref[:half] + a1_ref[...].astype(jnp.float32) + a2_ref[...].astype(jnp.float32)
    low = base_ref[half:] + b1_ref[...].astype(jnp.float32) + b2_ref[...].astype(jnp.float32)
    rows = jnp.concatenate([top, low], axis=0).astype(jnp.bfloat16)
    total_ref[...] = jnp.dot(rows, weight_ref[...], preferred_element_type=jnp.float32)
    lane = lane_ref[0]
    for offset, ref in ((2, o0), (1, o1), (3, o2), (0, own)):
        start = pl.multiple_of(((lane + offset) & 3) * part, part)
        ref[...] = total_ref[pl.ds(start, part)].astype(ref.dtype)


def project(lane, base, a1, a2, b1, b2, weight):
    count, width = base.shape
    part = count // 4
    vmem = pl.BlockSpec(memory_space=pltpu.VMEM)
    return pl.pallas_call(
        project_kernel,
        in_specs=[pl.BlockSpec(memory_space=pltpu.SMEM)] + [vmem] * 6,
        out_specs=[vmem] * 4,
        out_shape=[jax.ShapeDtypeStruct((part, width), jnp.bfloat16)] * 3
        + [jax.ShapeDtypeStruct((part, width), jnp.float32)],
        scratch_shapes=[pltpu.VMEM((count, width), jnp.float32)],
        compiler_params=pltpu.CompilerParams(vmem_limit_bytes=24 * MIB),
        cost_estimate=pl.CostEstimate(
            flops=2 * count * width * width,
            bytes_accessed=2 * width * width + 12 * count * width,
            transcendentals=0,
        ),
        name="project",
    )(lane, base, a1, a2, b1, b2, weight)


def turn(column):
    count = column.shape[0]
    same = lax.broadcasted_iota(jnp.int32, (count, count), 0) == lax.broadcasted_iota(
        jnp.int32, (count, count), 1
    )
    return jnp.sum(jnp.where(same, column, 0), axis=0, keepdims=True)


def route_kernel(
    lane_ref, own_ref, r0, r1, r2, counts_ref, owners_ref, dest_ref, seg_ref, out_ref
):
    lane = lane_ref[0]
    rows, width = own_ref.shape
    pieces = counts_ref.shape[1]
    slots = 2 * rows // pieces
    projected = (
        own_ref[...]
        + r0[...].astype(jnp.float32)
        + r1[...].astype(jnp.float32)
        + r2[...].astype(jnp.float32)
    ).astype(jnp.bfloat16)
    counts = counts_ref[...] // 4
    earlier = lax.broadcasted_iota(jnp.int32, (pieces, pieces), 1) < lax.broadcasted_iota(
        jnp.int32, (pieces, pieces), 0
    )
    starts = jnp.sum(jnp.where(earlier, counts, 0), axis=1, keepdims=True)
    upto = earlier | (
        lax.broadcasted_iota(jnp.int32, (pieces, pieces), 1)
        == lax.broadcasted_iota(jnp.int32, (pieces, pieces), 0)
    )
    ends = jnp.sum(jnp.where(upto, counts, 0), axis=1, keepdims=True)
    index = lax.broadcasted_iota(jnp.int32, (pieces, rows), 1)
    inside = (index >= starts) & (index < ends)
    owner_col = jnp.sum(
        jnp.where(
            lax.broadcasted_iota(jnp.int32, (pieces, pieces), 0)
            == lax.broadcasted_iota(jnp.int32, (pieces, pieces), 1),
            owners_ref[...],
            0,
        ),
        axis=1,
        keepdims=True,
    )
    target = jnp.sum(jnp.where(inside, owner_col * slots - starts, 0), axis=0, keepdims=True)
    target = target + lax.broadcasted_iota(jnp.int32, (1, rows), 1)
    out_rows = pieces * slots
    hits = lax.broadcasted_iota(jnp.int32, (out_rows, rows), 0) == target
    moved = jnp.dot(
        jnp.where(hits, 1.0, 0.0).astype(jnp.bfloat16),
        projected,
        preferred_element_type=jnp.float32,
    ).astype(jnp.bfloat16)
    dest = dest_ref[lane]
    seg = seg_ref[lane]
    tokens = dest.shape[1]
    first = dest == 4 * lax.broadcasted_iota(jnp.int32, (rows, tokens), 0)
    marks = turn(jnp.sum(jnp.where(first, seg, 0), axis=1, keepdims=True)) + 1
    tags = jnp.sum(jnp.where(hits, marks, 0), axis=1, keepdims=True)
    out_ref[:, :width] = moved
    out_ref[:, width:] = jnp.broadcast_to(
        tags.astype(jnp.float32), (out_rows, out_ref.shape[1] - width)
    ).astype(jnp.bfloat16)


def route(lane, own, others, lengths, owners, merge_dest, segment_ids):
    rows, width = own.shape
    pieces = lengths.shape[0]
    block = merge_dest.shape[0] // 4
    vmem = pl.BlockSpec(memory_space=pltpu.VMEM)
    return pl.pallas_call(
        route_kernel,
        in_specs=[pl.BlockSpec(memory_space=pltpu.SMEM)] + [vmem] * 8,
        out_specs=vmem,
        out_shape=jax.ShapeDtypeStruct((2 * rows, width + 128), jnp.bfloat16),
        compiler_params=pltpu.CompilerParams(vmem_limit_bytes=24 * MIB),
        name="route",
    )(
        lane,
        own,
        *others,
        lengths.reshape(1, pieces),
        owners.reshape(1, pieces),
        merge_dest.reshape(4, 1, block),
        segment_ids.reshape(4, 1, block),
    )


def pack_kernel(core_ref, weight_ref, keep_ref, send_ref):
    core = core_ref[0]
    parts, _, width = weight_ref.shape
    half = width // 2
    keep_ref[:, parts * half :] = jnp.zeros_like(keep_ref[:, parts * half :])
    send_ref[:, parts * half :] = jnp.zeros_like(send_ref[:, parts * half :])
    for part in range(parts):
        low = weight_ref[part, :, :half]
        high = weight_ref[part, :, half:]
        at = slice(part * half, (part + 1) * half)

        @pl.when(core == 0)
        def _():
            keep_ref[:, at] = low
            send_ref[:, at] = high

        @pl.when(core == 1)
        def _():
            keep_ref[:, at] = high
            send_ref[:, at] = low


def pack(core, weight):
    parts, depth, width = weight.shape
    columns = parts * width // 2 + 64
    return pl.pallas_call(
        pack_kernel,
        in_specs=[SMEM, VMEM],
        out_specs=[VMEM] * 2,
        out_shape=[jax.ShapeDtypeStruct((depth, columns), jnp.bfloat16)] * 2,
        compiler_params=pltpu.CompilerParams(vmem_limit_bytes=8 * MIB),
        name="pack",
    )(core, weight)


def pair_kernel(core_ref, own_ref, other_ref, *out_refs):
    core = core_ref[0]
    depth = own_ref.shape[0]
    size = out_refs[0].shape[2]
    index = lax.broadcasted_iota(jnp.int32, (2 * depth, depth), 0)
    column = lax.broadcasted_iota(jnp.int32, (2 * depth, depth), 1)
    own_hits = jnp.where(index == column + core * depth, 1.0, 0.0).astype(jnp.bfloat16)
    other_hits = jnp.where(index == column + (1 - core) * depth, 1.0, 0.0).astype(jnp.bfloat16)
    both = jnp.dot(own_hits, own_ref[...], preferred_element_type=jnp.float32) + jnp.dot(
        other_hits, other_ref[...], preferred_element_type=jnp.float32
    )
    both = both.astype(jnp.bfloat16)
    for i, ref in enumerate(out_refs):
        ref[0] = both[:, i * size : (i + 1) * size]


def pair(core, own, other, streams):
    depth, columns = own.shape
    return pl.pallas_call(
        pair_kernel,
        in_specs=[SMEM, VMEM, VMEM],
        out_specs=[VMEM] * streams,
        out_shape=[jax.ShapeDtypeStruct((1, 2 * depth, columns // streams), jnp.bfloat16)]
        * streams,
        compiler_params=pltpu.CompilerParams(vmem_limit_bytes=8 * MIB),
        name="pair",
    )(core, own, other)


ORDERS = ((1, 4, 3, 12), (4, 3, 12, 1), (3, 12, 1, 4), (12, 1, 4, 3))


def assemble(chip, streams, chips):
    _, depth, size = streams[0][0].shape

    def kernel(chip_ref, *refs):
        out_ref = refs[-1]
        chip_id = chip_ref[0]
        for s, order in enumerate(ORDERS):
            d1, d2, d3, d4 = order
            inner = (0, d1, d2, d2 ^ d1)
            for a, outer in enumerate((0, d3, d4, d4 ^ d3)):
                for i, mask in enumerate(inner):
                    out_ref[chip_id ^ (outer ^ mask), :, s * size : (s + 1) * size] = refs[
                        4 * s + a
                    ][i]

    flat = [array for stream in streams for array in stream]
    return pl.pallas_call(
        kernel,
        in_specs=[SMEM] + [VMEM] * len(flat),
        out_specs=VMEM,
        out_shape=jax.ShapeDtypeStruct((chips, depth, size * len(ORDERS)), jnp.bfloat16),
        compiler_params=pltpu.CompilerParams(vmem_limit_bytes=30 * MIB),
        cost_estimate=pl.CostEstimate(flops=0, bytes_accessed=1 << 24, transcendentals=0),
        name="assemble",
    )(chip, *flat)


def attention(heads_ref, base, tags, count, width, out_ref):
    tag_col = tags
    itself = lax.broadcasted_iota(jnp.int32, (count, count), 0) == lax.broadcasted_iota(
        jnp.int32, (count, count), 1
    )
    tag_row = jnp.sum(jnp.where(itself, tag_col, 0.0), axis=0, keepdims=True)
    allowed = ((tag_col == tag_row) & (tag_row > 0.5)) | itself
    live = tag_col > 0.5
    scale = 1.0 / math.sqrt(HEAD_DIM)
    rows = slice(base, base + count)
    for head in range(width // HEAD_DIM):
        at = head * HEAD_DIM
        query = heads_ref[rows, at : at + HEAD_DIM]
        keys = heads_ref[rows, width + at : width + at + HEAD_DIM]
        value = heads_ref[rows, 2 * width + at : 2 * width + at + HEAD_DIM]
        scores = (
            lax.dot_general(
                query, keys, (((1,), (1,)), ((), ())), preferred_element_type=jnp.float32
            )
            * scale
        )
        weights = jnp.where(allowed, jnp.exp(scores), 0.0)
        probs = (weights / jnp.sum(weights, axis=-1, keepdims=True)).astype(jnp.bfloat16)
        mixed = jnp.dot(probs, value, preferred_element_type=jnp.float32)
        out_ref[:, at : at + HEAD_DIM] = jnp.where(live, mixed, 0.0).astype(jnp.bfloat16)


def attend_kernel(
    core_ref,
    mine_ref,
    theirs_ref,
    gain_ref,
    bias_ref,
    weight_ref,
    merged_ref,
    other_ref,
    heads_out_ref,
    tags_ref,
    heads_ref,
):
    core = core_ref[0]
    count, width = merged_ref.shape
    target = lax.broadcasted_iota(jnp.int32, (count, count), 0)
    source = lax.broadcasted_iota(jnp.int32, (count, count), 1)
    from_mine = ((target >> 2) & 1) == core

    def one_hot(hits):
        return jnp.where(hits, 1.0, 0.0).astype(jnp.bfloat16)

    def gather(first_hits, second_hits):
        return jnp.dot(
            one_hot(first_hits), mine_ref[...], preferred_element_type=jnp.float32
        ) + jnp.dot(one_hot(second_hits), theirs_ref[...], preferred_element_type=jnp.float32)

    same = target == source
    swapped = (target ^ 4) == source
    here = gather(from_mine & same, ~from_mine & swapped)
    there = gather(from_mine & swapped, ~from_mine & same)
    merged_ref[...] = here[:, :width].astype(jnp.bfloat16)
    both = jnp.concatenate([there, here], axis=0)
    normed = normalise(both[:, :width], gain_ref[...], bias_ref[...]).astype(jnp.bfloat16)
    heads_ref[...] = jnp.dot(normed, weight_ref[...], preferred_element_type=jnp.float32).astype(
        jnp.bfloat16
    )
    heads_out_ref[...] = heads_ref[count:]
    tags_ref[...] = here[:, width:]
    attention(heads_ref, 0, there[:, width : width + 1], count, width // 2, other_ref)


def attend_own_kernel(heads_ref, tags_ref, out_ref):
    attention(heads_ref, 0, tags_ref[:, :1], *out_ref.shape, out_ref)


def finish_kernel(core_ref, mine_ref, theirs_ref, out_ref):
    core = core_ref[0]
    half = mine_ref.shape[1]

    @pl.when(core == 0)
    def _():
        out_ref[:, :half] = mine_ref[...]
        out_ref[:, half:] = theirs_ref[...]

    @pl.when(core == 1)
    def _():
        out_ref[:, :half] = theirs_ref[...]
        out_ref[:, half:] = mine_ref[...]


def attend(core, mine, theirs, gain, bias, weight, sibling):
    count = mine.shape[0]
    width, columns = weight.shape
    bf16 = jnp.bfloat16
    merged, other, heads, tags = pl.pallas_call(
        attend_kernel,
        in_specs=[SMEM] + [VMEM] * 5,
        out_specs=[VMEM] * 4,
        out_shape=[
            jax.ShapeDtypeStruct((count, width), bf16),
            jax.ShapeDtypeStruct((count, width // 2), bf16),
            jax.ShapeDtypeStruct((count, columns), bf16),
            jax.ShapeDtypeStruct((count, mine.shape[1] - width), jnp.float32),
        ],
        scratch_shapes=[pltpu.VMEM((2 * count, columns), bf16)],
        compiler_params=pltpu.CompilerParams(vmem_limit_bytes=24 * MIB),
        name="attend",
    )(core, mine, theirs, gain, bias, weight)
    other = lax.ppermute(other, "req", sibling)
    own = pl.pallas_call(
        attend_own_kernel,
        in_specs=[VMEM] * 2,
        out_specs=VMEM,
        out_shape=jax.ShapeDtypeStruct((count, width // 2), bf16),
        compiler_params=pltpu.CompilerParams(vmem_limit_bytes=12 * MIB),
        cost_estimate=pl.CostEstimate(flops=1 << 30, bytes_accessed=1 << 20, transcendentals=0),
        name="attend_own",
    )(heads, tags)
    mixed = pl.pallas_call(
        finish_kernel,
        in_specs=[SMEM, VMEM, VMEM],
        out_specs=VMEM,
        out_shape=jax.ShapeDtypeStruct((count, width), bf16),
        compiler_params=pltpu.CompilerParams(vmem_limit_bytes=4 * MIB),
        name="finish",
    )(core, own, other)
    return merged, mixed


def body(
    residual_in,
    lengths,
    owners,
    merge_dest,
    segment_ids,
    norm2_gain,
    norm2_bias,
    up_weight,
    up_bias,
    down_weight,
    down_bias,
    proj_weight,
    norm3_gain,
    norm3_bias,
    next_weight,
):
    width = residual_in.shape[1]
    lanes = lax.axis_size("mlp")
    lane = lax.axis_index("mlp").astype(jnp.int32).reshape(1)
    onward = [(i, (i + 1) % lanes) for i in range(lanes)]
    back = [(i, (i - 1) % lanes) for i in range(lanes)]
    across = [(i, (i + 2) % lanes) for i in range(lanes)]

    def row(vector):
        return vector.reshape(1, -1)

    count = residual_in.shape[0] // lanes
    bias_up = row(up_bias)
    place = lax.axis_index("req").astype(jnp.int32)
    core = (place & 1).reshape(1)
    chip = (place >> 1).reshape(1)
    senders = lax.axis_size("req")
    sibling = [(i, i ^ 1) for i in range(senders)]

    def swap(array, mask):
        return lax.ppermute(array, "req", [(i, i ^ (2 * mask)) for i in range(senders)])

    keep, send = pack(core, next_weight.transpose(1, 0, 2))
    chunks = pair(core, keep, lax.ppermute(send, "req", sibling), len(ORDERS))
    got1 = [swap(chunks[s], order[0]) for s, order in enumerate(ORDERS)]
    far_a, far_b, normed, own_rows = first(
        lane,
        residual_in,
        merge_dest,
        row(norm2_gain),
        row(norm2_bias),
        up_weight,
        bias_up,
        down_weight,
    )
    got2 = [
        (swap(chunks[s], order[1]), swap(got1[s], order[1])) for s, order in enumerate(ORDERS)
    ]
    quads = [
        jnp.concatenate([chunks[s], got1[s], got2[s][0], got2[s][1]], axis=0)
        for s in range(len(ORDERS))
    ]
    got3 = [swap(quads[s], order[2]) for s, order in enumerate(ORDERS)]
    got4 = [
        (swap(quads[s], order[3]), swap(got3[s], order[3])) for s, order in enumerate(ORDERS)
    ]
    far_a = lax.ppermute(far_a, "mlp", onward)
    far_b = lax.ppermute(far_b, "mlp", back)
    next_a, next_b = feed(normed, 0, up_weight, bias_up, down_weight)
    b1 = lax.ppermute(next_b, "mlp", onward)
    prev_a, prev_b = feed(normed, 1, up_weight, bias_up, down_weight)
    a2 = lax.ppermute(prev_a, "mlp", back)

    def join(first, second):
        return (first.astype(jnp.float32) + second.astype(jnp.float32)).astype(jnp.bfloat16)

    a1 = lax.ppermute(join(far_a, next_a), "mlp", onward)
    b2 = lax.ppermute(join(far_b, prev_b), "mlp", back)
    base = feed(
        normed,
        2,
        up_weight,
        bias_up,
        down_weight,
        (own_rows, row(down_bias)),
    )
    p0, p1, p2, own = project(lane, base, a1, a2, b1, b2, proj_weight)
    others = (
        lax.ppermute(p0, "mlp", across),
        lax.ppermute(p1, "mlp", onward),
        lax.ppermute(p2, "mlp", back),
    )
    outgoing = route(lane, own, others, lengths, owners, merge_dest, segment_ids)
    groups = [[2 * i + c for i in range(senders // 2)] for c in range(2)]
    mine = lax.all_to_all(
        outgoing, "req", split_axis=0, concat_axis=0, axis_index_groups=groups, tiled=True
    )
    theirs = lax.ppermute(mine, "req", sibling)
    full = assemble(
        chip,
        [
            (quads[s], got3[s], got4[s][0], got4[s][1])
            for s in range(len(ORDERS))
        ],
        senders // 2,
    )
    return attend(
        core,
        mine,
        theirs,
        row(norm3_gain),
        row(norm3_bias),
        full.reshape(width, -1),
        sibling,
    )


def solution(mesh):
    return jax.shard_map(
        body,
        mesh=mesh,
        in_specs=(
            P("req", None),
            P(("req", "mlp")),
            P(("req", "mlp")),
            P("req"),
            P("req"),
            P(),
            P(),
            P("mlp", None),
            P("mlp"),
            P("mlp", None),
            P(),
            P("mlp", None),
            P(),
            P(),
            P("req", None, None),
        ),
        out_specs=(P(("req", "mlp"), None), P(("req", "mlp"), None)),
        check_vma=False,
    )
```

```python
import math

import jax
import jax.numpy as jnp
from jax import lax
from jax.experimental import pallas as pl
from jax.experimental.pallas import tpu as pltpu
from jax.sharding import PartitionSpec as P

HEAD_DIM = 104
EPSILON = 1e-06
MIB = 1 << 20


def normalise(values, gain, bias):
    mean_value = jnp.mean(values, axis=-1, keepdims=True)
    centred = values - mean_value
    spread = jnp.mean(centred * centred, axis=-1, keepdims=True)
    return centred * lax.rsqrt(spread + EPSILON) * gain + bias


def relative_offset(step):
    return jnp.where(step == 0, 2, jnp.where(step == 1, 1, jnp.where(step == 2, 3, 0)))


def gelu(value):
    return 0.5 * value * (1.0 + lax.erf(value * (1.0 / math.sqrt(2.0))))


def feed_tiles(rows, up_ref, up_bias_ref, down_ref, tile=256):
    total = None
    for at in range(0, up_ref.shape[0], tile):
        upward = lax.dot_general(
            rows,
            up_ref[at : at + tile],
            (((1,), (1,)), ((), ())),
            preferred_element_type=jnp.float32,
        )
        hidden = gelu(upward + up_bias_ref[:, at : at + tile]).astype(jnp.bfloat16)
        part = jnp.dot(hidden, down_ref[at : at + tile], preferred_element_type=jnp.float32)
        total = part if total is None else total + part
    return total


def arrange_kernel(
    lane_ref,
    rows_hbm,
    dest_ref,
    gain_ref,
    bias_ref,
    up_hbm,
    down_hbm,
    normed_ref,
    own_ref,
    up_ref,
    down_ref,
    rows_ref,
    row_sems,
    sems,
):
    lane = lane_ref[0]
    count = rows_hbm.shape[0] // 4
    part = count // 4
    row_copies = [
        pltpu.make_async_copy(
            rows_hbm.at[pl.ds(i * count, count)],
            rows_ref.at[pl.ds(i * count, count)],
            row_sems.at[i],
        )
        for i in range(4)
    ]
    up_copy = pltpu.make_async_copy(up_hbm, up_ref, sems.at[0])
    down_copy = pltpu.make_async_copy(down_hbm, down_ref, sems.at[1])
    for copy in row_copies:
        copy.start()
    up_copy.start()
    down_copy.start()
    index = lax.broadcasted_iota(jnp.int32, (count, count), 0)
    step = index // part
    wanted = 4 * (index - step * part) + ((lane + relative_offset(step)) & 3)
    for b in range(4):
        row_copies[b].wait()
        rows = rows_ref[b * count : (b + 1) * count]
        normed = normalise(rows.astype(jnp.float32), gain_ref[...], bias_ref[...])
        hits = jnp.where(dest_ref[b] == wanted, 1.0, 0.0).astype(jnp.bfloat16)
        moved = jnp.dot(
            hits, normed.astype(jnp.bfloat16), preferred_element_type=jnp.float32
        ).astype(jnp.bfloat16)
        for k in range(4):
            normed_ref[k, b * part : (b + 1) * part] = moved[k * part : (k + 1) * part]
        own_ref[b * part : (b + 1) * part] = jnp.dot(
            hits[3 * part :], rows, preferred_element_type=jnp.float32
        ).astype(jnp.bfloat16)
    up_copy.wait()
    down_copy.wait()


VMEM = pl.BlockSpec(memory_space=pltpu.VMEM)
SMEM = pl.BlockSpec(memory_space=pltpu.SMEM)
HBM = pl.BlockSpec(memory_space=pltpu.HBM)


def in_hbm(array):
    return pltpu.with_memory_space_constraint(array, pltpu.HBM)


def arrange(lane, residual_in, merge_dest, gain, bias, up_weight, down_weight):
    group_rows, width = residual_in.shape
    count = group_rows // 4
    bf16 = jnp.bfloat16
    return pl.pallas_call(
        arrange_kernel,
        in_specs=[SMEM, HBM, VMEM, VMEM, VMEM, HBM, HBM],
        out_specs=[VMEM] * 4,
        out_shape=[
            pltpu.VMEM((4, count, width), bf16),
            pltpu.VMEM((count, width), bf16),
            pltpu.VMEM(up_weight.shape, bf16),
            pltpu.VMEM(down_weight.shape, bf16),
        ],
        scratch_shapes=[
            pltpu.VMEM(residual_in.shape, bf16),
            pltpu.SemaphoreType.DMA((4,)),
            pltpu.SemaphoreType.DMA((2,)),
        ],
        compiler_params=pltpu.CompilerParams(vmem_limit_bytes=16 * MIB),
        cost_estimate=FEED_COST,
        name="arrange",
    )(
        lane,
        in_hbm(residual_in),
        merge_dest.reshape(4, 1, count),
        gain,
        bias,
        in_hbm(up_weight),
        in_hbm(down_weight),
    )


def feed_kernel(rows_ref, up_ref, up_bias_ref, down_ref, *out_refs):
    total = feed_tiles(rows_ref[...], up_ref, up_bias_ref, down_ref)
    size = out_refs[0].shape[0]
    for i, ref in enumerate(out_refs):
        ref[...] = total[i * size : (i + 1) * size].astype(jnp.bfloat16)


def feed_own_kernel(
    rows_ref, up_ref, up_bias_ref, down_ref, residual_ref, down_bias_ref, out_ref
):
    total = feed_tiles(rows_ref[...], up_ref, up_bias_ref, down_ref)
    out_ref[...] = total + (residual_ref[...].astype(jnp.float32) + down_bias_ref[...])


FEED_COST = pl.CostEstimate(flops=1 << 20, bytes_accessed=1 << 16, transcendentals=0)


def feed(rows, step, up_weight, up_bias, down_weight, extra=None, pieces=1):
    _, count, width = rows.shape
    args = [rows, up_weight, up_bias, down_weight]
    if extra is None:
        out_shape = [jax.ShapeDtypeStruct((count // pieces, width), jnp.bfloat16)] * pieces
        kernel = feed_kernel
    else:
        args += list(extra)
        out_shape = jax.ShapeDtypeStruct((count, width), jnp.float32)
        kernel = feed_own_kernel

    def wrapped(rows_ref, *refs):
        kernel(rows_ref.at[step], *refs)

    return pl.pallas_call(
        wrapped,
        in_specs=[VMEM] * len(args),
        out_specs=[VMEM] * pieces if extra is None else VMEM,
        out_shape=out_shape,
        compiler_params=pltpu.CompilerParams(vmem_limit_bytes=16 * MIB),
        cost_estimate=FEED_COST,
        name="feed",
    )(*args)


def project_kernel(
    lane_ref,
    base_ref,
    onward_top,
    onward_low,
    back_top,
    back_low,
    weight_ref,
    fa,
    fb,
    following,
    previous,
    own,
    total_ref,
):
    split = onward_top.shape[0]
    top = base_ref[:split] + onward_top[...].astype(jnp.float32) + back_top[...].astype(jnp.float32)
    low = base_ref[split:] + onward_low[...].astype(jnp.float32) + back_low[...].astype(jnp.float32)
    rows = jnp.concatenate([top, low], axis=0)
    total_ref[...] = jnp.dot(
        rows.astype(jnp.bfloat16), weight_ref[...], preferred_element_type=jnp.float32
    )
    lane = lane_ref[0]
    half = fa.shape[0]
    part = 2 * half

    def block(offset, at, size):
        start = pl.multiple_of(((lane + offset) & 3) * part + at, half)
        return total_ref[pl.ds(start, size)]

    fa[...] = block(2, 0, half).astype(jnp.bfloat16)
    fb[...] = block(2, half, half).astype(jnp.bfloat16)
    following[...] = block(1, 0, part).astype(jnp.bfloat16)
    previous[...] = block(3, 0, part).astype(jnp.bfloat16)
    own[...] = block(0, 0, part)


def project(lane, base, halves, weight):
    count, width = base.shape
    part = count // 4
    bf16 = jnp.bfloat16
    return pl.pallas_call(
        project_kernel,
        in_specs=[SMEM] + [VMEM] * 6,
        out_specs=[VMEM] * 5,
        out_shape=[jax.ShapeDtypeStruct((part // 2, width), bf16)] * 2
        + [jax.ShapeDtypeStruct((part, width), bf16)] * 2
        + [jax.ShapeDtypeStruct((part, width), jnp.float32)],
        scratch_shapes=[pltpu.VMEM((count, width), jnp.float32)],
        compiler_params=pltpu.CompilerParams(vmem_limit_bytes=16 * MIB),
        cost_estimate=FEED_COST,
        name="project",
    )(lane, base, *halves, weight)


def turn(column):
    count = column.shape[0]
    same = lax.broadcasted_iota(jnp.int32, (count, count), 0) == lax.broadcasted_iota(
        jnp.int32, (count, count), 1
    )
    return jnp.sum(jnp.where(same, column, 0), axis=0, keepdims=True)


def route_kernel(
    lane_ref, own_ref, r0, r1, counts_ref, owners_ref, dest_ref, seg_ref, out_ref
):
    lane = lane_ref[0]
    rows, width = own_ref.shape
    pieces = counts_ref.shape[1]
    slots = 2 * rows // pieces
    projected = (
        own_ref[...]
        + r0[...].astype(jnp.float32)
        + r1[...].astype(jnp.float32)
    ).astype(jnp.bfloat16)
    counts = counts_ref[...] // 4
    earlier = lax.broadcasted_iota(jnp.int32, (pieces, pieces), 1) < lax.broadcasted_iota(
        jnp.int32, (pieces, pieces), 0
    )
    starts = jnp.sum(jnp.where(earlier, counts, 0), axis=1, keepdims=True)
    upto = earlier | (
        lax.broadcasted_iota(jnp.int32, (pieces, pieces), 1)
        == lax.broadcasted_iota(jnp.int32, (pieces, pieces), 0)
    )
    ends = jnp.sum(jnp.where(upto, counts, 0), axis=1, keepdims=True)
    index = lax.broadcasted_iota(jnp.int32, (pieces, rows), 1)
    inside = (index >= starts) & (index < ends)
    owner_col = jnp.sum(
        jnp.where(
            lax.broadcasted_iota(jnp.int32, (pieces, pieces), 0)
            == lax.broadcasted_iota(jnp.int32, (pieces, pieces), 1),
            owners_ref[...],
            0,
        ),
        axis=1,
        keepdims=True,
    )
    target = jnp.sum(jnp.where(inside, owner_col * slots - starts, 0), axis=0, keepdims=True)
    target = target + lax.broadcasted_iota(jnp.int32, (1, rows), 1)
    out_rows = pieces * slots
    hits = lax.broadcasted_iota(jnp.int32, (out_rows, rows), 0) == target
    moved = jnp.dot(
        jnp.where(hits, 1.0, 0.0).astype(jnp.bfloat16),
        projected,
        preferred_element_type=jnp.float32,
    ).astype(jnp.bfloat16)
    dest = dest_ref[lane]
    seg = seg_ref[lane]
    tokens = dest.shape[1]
    first = dest == 4 * lax.broadcasted_iota(jnp.int32, (rows, tokens), 0)
    marks = turn(jnp.sum(jnp.where(first, seg, 0), axis=1, keepdims=True)) + 1
    tags = jnp.sum(jnp.where(hits, marks, 0), axis=1, keepdims=True)
    out_ref[:, :width] = moved
    out_ref[:, width:] = jnp.broadcast_to(
        tags.astype(jnp.float32), (out_rows, out_ref.shape[1] - width)
    ).astype(jnp.bfloat16)


def route(lane, own, others, lengths, owners, merge_dest, segment_ids):
    rows, width = own.shape
    pieces = lengths.shape[0]
    block = merge_dest.shape[0] // 4
    return pl.pallas_call(
        route_kernel,
        in_specs=[SMEM] + [VMEM] * 7,
        out_specs=VMEM,
        out_shape=jax.ShapeDtypeStruct((2 * rows, width + 128), jnp.bfloat16),
        compiler_params=pltpu.CompilerParams(vmem_limit_bytes=24 * MIB),
        name="route",
    )(
        lane,
        own,
        *others,
        lengths.reshape(1, pieces),
        owners.reshape(1, pieces),
        merge_dest.reshape(4, 1, block),
        segment_ids.reshape(4, 1, block),
    )


def pack_kernel(core_ref, weight_ref, keep_ref, send_ref):
    core = core_ref[0]
    parts, _, width = weight_ref.shape
    half = width // 2
    keep_ref[:, parts * half :] = jnp.zeros_like(keep_ref[:, parts * half :])
    send_ref[:, parts * half :] = jnp.zeros_like(send_ref[:, parts * half :])
    for part in range(parts):
        low = weight_ref[part, :, :half]
        high = weight_ref[part, :, half:]
        at = slice(part * half, (part + 1) * half)

        @pl.when(core == 0)
        def _():
            keep_ref[:, at] = low
            send_ref[:, at] = high

        @pl.when(core == 1)
        def _():
            keep_ref[:, at] = high
            send_ref[:, at] = low


def pack(core, weight):
    parts, depth, width = weight.shape
    columns = parts * width // 2 + 64
    return pl.pallas_call(
        pack_kernel,
        in_specs=[SMEM, VMEM],
        out_specs=[VMEM] * 2,
        out_shape=[jax.ShapeDtypeStruct((depth, columns), jnp.bfloat16)] * 2,
        compiler_params=pltpu.CompilerParams(vmem_limit_bytes=8 * MIB),
        name="pack",
    )(core, weight)


def pair_kernel(core_ref, own_ref, other_ref, *out_refs):
    core = core_ref[0]
    depth = own_ref.shape[0]
    size = out_refs[0].shape[2]
    index = lax.broadcasted_iota(jnp.int32, (2 * depth, depth), 0)
    column = lax.broadcasted_iota(jnp.int32, (2 * depth, depth), 1)
    own_hits = jnp.where(index == column + core * depth, 1.0, 0.0).astype(jnp.bfloat16)
    other_hits = jnp.where(index == column + (1 - core) * depth, 1.0, 0.0).astype(jnp.bfloat16)
    both = jnp.dot(own_hits, own_ref[...], preferred_element_type=jnp.float32) + jnp.dot(
        other_hits, other_ref[...], preferred_element_type=jnp.float32
    )
    both = both.astype(jnp.bfloat16)
    for i, ref in enumerate(out_refs):
        ref[0] = both[:, i * size : (i + 1) * size]


def pair(core, own, other, streams):
    depth, columns = own.shape
    return pl.pallas_call(
        pair_kernel,
        in_specs=[SMEM, VMEM, VMEM],
        out_specs=[VMEM] * streams,
        out_shape=[jax.ShapeDtypeStruct((1, 2 * depth, columns // streams), jnp.bfloat16)]
        * streams,
        compiler_params=pltpu.CompilerParams(vmem_limit_bytes=8 * MIB),
        name="pair",
    )(core, own, other)


ORDERS = (((1, 4, 3, 12), (4, 3, 12, 1)), ((3, 12, 1, 4), (12, 1, 4, 3)))


def masks(order):
    found = [0]
    for bit in order:
        found += [bit ^ mask for mask in found]
    return found


def assemble(chip, core, streams, chips):
    held, depth, size = streams[0][0].shape
    arrays = len(streams[0])

    def kernel(chip_ref, core_ref, *refs):
        *held_refs, out_ref, token_ref, sems = refs
        chip_id = chip_ref[0]
        core_id = core_ref[0]
        copies = []
        for s, orders in enumerate(ORDERS):
            for i, (low, high) in enumerate(zip(masks(orders[0]), masks(orders[1]))):
                at = chip_id ^ jnp.where(core_id == 0, low, high)
                copies.append(
                    pltpu.make_async_copy(
                        held_refs[arrays * s + i // held].at[i % held],
                        out_ref.at[at, :, pl.ds(s * size, size)],
                        sems.at[len(copies)],
                    )
                )
        for copy in copies:
            copy.start()
        for copy in copies:
            copy.wait()
        token_ref[...] = jnp.zeros_like(token_ref)

    flat = [in_hbm(array) for stream in streams for array in stream]
    return pl.pallas_call(
        kernel,
        in_specs=[SMEM, SMEM] + [HBM] * len(flat),
        out_specs=[VMEM, VMEM],
        out_shape=[
            pltpu.VMEM((chips, depth, size * len(ORDERS)), jnp.bfloat16),
            jax.ShapeDtypeStruct((8, 128), jnp.float32),
        ],
        scratch_shapes=[pltpu.SemaphoreType.DMA((chips * len(ORDERS),))],
        compiler_params=pltpu.CompilerParams(vmem_limit_bytes=4 * MIB),
        cost_estimate=pl.CostEstimate(flops=1 << 30, bytes_accessed=1 << 24, transcendentals=0),
        name="assemble",
    )(chip, core, *flat)


def attention(heads_ref, base, tags, count, width, out_ref):
    tag_col = tags
    itself = lax.broadcasted_iota(jnp.int32, (count, count), 0) == lax.broadcasted_iota(
        jnp.int32, (count, count), 1
    )
    tag_row = jnp.sum(jnp.where(itself, tag_col, 0.0), axis=0, keepdims=True)
    allowed = ((tag_col == tag_row) & (tag_row > 0.5)) | itself
    live = tag_col > 0.5
    scale = 1.0 / math.sqrt(HEAD_DIM)
    rows = slice(base, base + count)
    for head in range(width // HEAD_DIM):
        at = head * HEAD_DIM
        query = heads_ref[rows, at : at + HEAD_DIM]
        keys = heads_ref[rows, width + at : width + at + HEAD_DIM]
        value = heads_ref[rows, 2 * width + at : 2 * width + at + HEAD_DIM]
        scores = (
            lax.dot_general(
                query, keys, (((1,), (1,)), ((), ())), preferred_element_type=jnp.float32
            )
            * scale
        )
        weights = jnp.where(allowed, jnp.exp(scores), 0.0)
        probs = (weights / jnp.sum(weights, axis=-1, keepdims=True)).astype(jnp.bfloat16)
        mixed = jnp.dot(probs, value, preferred_element_type=jnp.float32)
        out_ref[:, at : at + HEAD_DIM] = jnp.where(live, mixed, 0.0).astype(jnp.bfloat16)


def attend_kernel(
    core_ref,
    mine_ref,
    theirs_ref,
    gain_ref,
    bias_ref,
    weight_ref,
    token_ref,
    merged_ref,
    other_ref,
    heads_out_ref,
    tags_ref,
    heads_ref,
):
    core = core_ref[0]
    count, width = merged_ref.shape
    target = lax.broadcasted_iota(jnp.int32, (count, count), 0)
    source = lax.broadcasted_iota(jnp.int32, (count, count), 1)
    from_mine = ((target >> 2) & 1) == core

    def one_hot(hits):
        return jnp.where(hits, 1.0, 0.0).astype(jnp.bfloat16)

    def gather(first_hits, second_hits):
        return jnp.dot(
            one_hot(first_hits), mine_ref[...], preferred_element_type=jnp.float32
        ) + jnp.dot(one_hot(second_hits), theirs_ref[...], preferred_element_type=jnp.float32)

    same = target == source
    swapped = (target ^ 4) == source
    here = gather(from_mine & same, ~from_mine & swapped)
    there = gather(from_mine & swapped, ~from_mine & same)
    merged_ref[...] = here[:, :width].astype(jnp.bfloat16)
    both = jnp.concatenate([there, here], axis=0)
    normed = normalise(both[:, :width], gain_ref[...], bias_ref[...]).astype(jnp.bfloat16)
    heads_ref[...] = jnp.dot(normed, weight_ref[...], preferred_element_type=jnp.float32).astype(
        jnp.bfloat16
    )
    heads_out_ref[...] = heads_ref[count:]
    tags_ref[...] = here[:, width:]
    attention(heads_ref, 0, there[:, width : width + 1], count, width // 2, other_ref)


def attend_own_kernel(heads_ref, tags_ref, out_ref):
    attention(heads_ref, 0, tags_ref[:, :1], *out_ref.shape, out_ref)


def finish_kernel(core_ref, mine_ref, theirs_ref, out_ref):
    core = core_ref[0]
    half = mine_ref.shape[1]

    @pl.when(core == 0)
    def _():
        out_ref[:, :half] = mine_ref[...]
        out_ref[:, half:] = theirs_ref[...]

    @pl.when(core == 1)
    def _():
        out_ref[:, :half] = theirs_ref[...]
        out_ref[:, half:] = mine_ref[...]


def attend(core, mine, theirs, gain, bias, weight, token, sibling):
    count = mine.shape[0]
    width, columns = weight.shape
    bf16 = jnp.bfloat16
    merged, other, heads, tags = pl.pallas_call(
        attend_kernel,
        in_specs=[SMEM] + [VMEM] * 5 + [pl.BlockSpec(memory_space=pl.ANY)],
        out_specs=[VMEM] * 4,
        out_shape=[
            jax.ShapeDtypeStruct((count, width), bf16),
            jax.ShapeDtypeStruct((count, width // 2), bf16),
            jax.ShapeDtypeStruct((count, columns), bf16),
            jax.ShapeDtypeStruct((count, mine.shape[1] - width), jnp.float32),
        ],
        scratch_shapes=[pltpu.VMEM((2 * count, columns), bf16)],
        compiler_params=pltpu.CompilerParams(vmem_limit_bytes=24 * MIB),
        name="attend",
    )(core, mine, theirs, gain, bias, weight, token)
    other = lax.ppermute(other, "req", sibling)
    own = pl.pallas_call(
        attend_own_kernel,
        in_specs=[VMEM] * 2,
        out_specs=VMEM,
        out_shape=jax.ShapeDtypeStruct((count, width // 2), bf16),
        compiler_params=pltpu.CompilerParams(vmem_limit_bytes=12 * MIB),
        cost_estimate=pl.CostEstimate(flops=1 << 30, bytes_accessed=1 << 20, transcendentals=0),
        name="attend_own",
    )(heads, tags)
    mixed = pl.pallas_call(
        finish_kernel,
        in_specs=[SMEM, VMEM, VMEM],
        out_specs=VMEM,
        out_shape=jax.ShapeDtypeStruct((count, width), bf16),
        compiler_params=pltpu.CompilerParams(vmem_limit_bytes=4 * MIB),
        name="finish",
    )(core, own, other)
    return merged, mixed


def body(
    residual_in,
    lengths,
    owners,
    merge_dest,
    segment_ids,
    norm2_gain,
    norm2_bias,
    up_weight,
    up_bias,
    down_weight,
    down_bias,
    proj_weight,
    norm3_gain,
    norm3_bias,
    next_weight,
):
    width = residual_in.shape[1]
    lanes = lax.axis_size("mlp")
    lane = lax.axis_index("mlp").astype(jnp.int32).reshape(1)
    onward = [(i, (i + 1) % lanes) for i in range(lanes)]
    back = [(i, (i - 1) % lanes) for i in range(lanes)]

    def row(vector):
        return vector.reshape(1, -1)

    count = residual_in.shape[0] // lanes
    bias_up = row(up_bias)
    place = lax.axis_index("req").astype(jnp.int32)
    core = (place & 1).reshape(1)
    chip = (place >> 1).reshape(1)
    senders = lax.axis_size("req")
    sibling = [(i, i ^ 1) for i in range(senders)]

    def swap(array, stream, step):
        partners = [i ^ (2 * ORDERS[stream][i & 1][step]) for i in range(senders)]
        return lax.ppermute(array, "req", list(enumerate(partners)))

    def step(arrays, index):
        return tuple(swap(array, s, index) for s, array in enumerate(arrays))

    tie = lax.optimization_barrier
    keep, send = pack(core, next_weight.transpose(1, 0, 2))
    keep, residual_in = tie((keep, residual_in))
    other = lax.ppermute(send, "req", sibling)
    normed, own_rows, up_weight, down_weight = arrange(
        lane, residual_in, merge_dest, norm2_gain, norm2_bias, up_weight, down_weight
    )

    def feed_step(index, *extra, pieces=1):
        return feed(normed, index, up_weight, bias_up, down_weight, *extra, pieces=pieces)

    other, normed = tie((other, normed))
    chunks = pair(core, keep, other, len(ORDERS))
    chunks, normed = tie((chunks, normed))
    got = step(chunks, 0)
    far_a, far_b = feed_step(0, pieces=2)
    got, normed = tie((got, normed))
    far_a = lax.ppermute(far_a, "mlp", onward)
    far_b = lax.ppermute(far_b, "mlp", back)
    two = tuple(jnp.concatenate(both, axis=0) for both in zip(chunks, got))
    two, normed = tie((two, normed))
    got2 = step(two, 1)
    f0, f1 = feed_step(1, pieces=2)
    p0, p1 = feed_step(2, pieces=2)
    base = feed_step(3, (own_rows, row(down_bias)))
    base, far_a, far_b, f0, f1, p0, p1, got2 = tie((base, far_a, far_b, f0, f1, p0, p1, got2))

    def join(first, second):
        return (first.astype(jnp.float32) + second.astype(jnp.float32)).astype(jnp.bfloat16)

    def hop(following, previous, far_a, far_b):
        half = far_a.shape[0]
        following = jnp.concatenate([join(following[:half], far_a), following[half:]], axis=0)
        previous = jnp.concatenate([previous[:half], join(previous[half:], far_b)], axis=0)
        return following, previous

    def shift(following, previous):
        return lax.ppermute(following, "mlp", onward), lax.ppermute(previous, "mlp", back)

    four = tuple(jnp.concatenate(both, axis=0) for both in zip(two, got2))
    joined = tie((join(f0, far_a), join(p1, far_b), four))
    onward_top, back_low = shift(*joined[:2])
    four = joined[2]
    got3 = step(four, 2)
    onward_top, back_low, got3, four, f1, p0 = tie((onward_top, back_low, got3, four, f1, p0))
    onward_low, back_top = shift(f1, p0)
    got4 = step(four, 3)
    halves = (onward_top, onward_low, back_top, back_low)
    halves, got4, got3 = tie((halves, got4, got3))
    got5 = step(got3, 3)
    far_a, far_b, following, previous, own = project(
        lane, base, halves, proj_weight
    )
    far_a = lax.ppermute(far_a, "mlp", onward)
    far_b = lax.ppermute(far_b, "mlp", back)
    following, previous = hop(following, previous, far_a, far_b)
    others = shift(following, previous)
    outgoing = route(lane, own, others, lengths, owners, merge_dest, segment_ids)
    groups = [[2 * i + c for i in range(senders // 2)] for c in range(2)]
    mine = lax.all_to_all(
        outgoing, "req", split_axis=0, concat_axis=0, axis_index_groups=groups, tiled=True
    )
    full, token = assemble(chip, core, list(zip(four, got3, got4, got5)), senders // 2)
    mine, token = tie((mine, token))
    theirs = lax.ppermute(mine, "req", sibling)
    return attend(
        core,
        mine,
        theirs,
        norm3_gain,
        norm3_bias,
        full.reshape(width, -1),
        token,
        sibling,
    )


def solution(mesh):
    return jax.shard_map(
        body,
        mesh=mesh,
        in_specs=(
            P("req", None),
            P(("req", "mlp")),
            P(("req", "mlp")),
            P("req"),
            P("req"),
            P(),
            P(),
            P("mlp", None),
            P("mlp"),
            P("mlp", None),
            P(),
            P("mlp", None),
            P(),
            P(),
            P("req", None, None),
        ),
        out_specs=(P(("req", "mlp"), None), P(("req", "mlp"), None)),
        check_vma=False,
    )
```
